256 devices in a mesh: seq: 4 (over z_hi), expert: 64 (over z_lo, y, x, core).
Axes of the slice: x: 4, y: 4, z: 8 (z_hi: 4, z_lo: 2; z = z_hi * 2 + z_lo), core: 2. Of those that a mesh axis runs over, the one named last changes fastest.
Arguments:
- tokens: bfloat16 [32768, 4096], P(('seq', 'expert')), may hold values from -6 to 6
- expert_ids: int32 [32768, 1], P(('seq', 'expert')), may hold values from 0 to 63; in each aligned block of 128 rows (0 to 127, 128 to 255, ...) at most 3 rows name the same one
- gate_weights: bfloat16 [32768, 1], P(('seq', 'expert')), may hold values from 0.049804688 to 1
- w_gate: bfloat16 [64, 768, 4096], P('expert', 'seq'), may hold values from -0.09375 to 0.09375
- w_up: bfloat16 [64, 768, 4096], P('expert', 'seq'), may hold values from -0.09375 to 0.09375
- w_down: bfloat16 [64, 768, 4096], P('expert', 'seq'), may hold values from -0.21875 to 0.21875
- cotangent: bfloat16 [32768, 4096], P(('seq', 'expert')), may hold values from -2 to 2
Outputs:
- d_tokens: bfloat16 [32768, 4096], P(('seq', 'expert'))
- d_gates: float32 [32768, 1], P(('seq', 'expert'))
- grad_gate: bfloat16 [64, 768, 4096], P('expert', 'seq')
- grad_up: bfloat16 [64, 768, 4096], P('expert', 'seq')
- grad_down: bfloat16 [64, 768, 4096], P('expert', 'seq')
The draws below stay inside these ranges and needn't reach their ends.
Inputs may be any that keep to these rules, and one draw needn't show every extreme that they name: `expert_ids`: each row names one expert. Among the rows of one device (aligned blocks of 128 rows) no expert is named more than 3 times, and in every draw some expert is named exactly 3 times in some block.
All inputs are finite; a program needn't handle non-finite values.
Results may differ from the reference program's by a relative error of at most 0.012.
Values may be sent and summed in bfloat16 or wider, within the bound.
No kernel may reach another device: no remote copies, remote signals or barrier semaphores. Data moves between devices by JAX's collectives and lax.ppermute only.
A program may use at most 192 MiB of HBM per device.

```python
import math
import jax
import jax.numpy as jnp
import numpy as np
from jax import lax

D = 4096
H = 768
TOPK = 1
TOK_DEV = 128
EXPERTS = 64
H_DEV = 192
CAP = 3
TOKENS = 32768
N_SEQ = 4


def steps_of(rng, dims, split, low, high):
    level, own = 1.0, jax.random.fold_in(rng, 6)
    for axis_at, shards_of in split:
        heights = jnp.exp(jax.random.uniform(jax.random.fold_in(own, axis_at), (shards_of,), jnp.float32, low / len(split), high / len(split)))
        level = level * jnp.repeat(heights, dims[axis_at] // shards_of).reshape([-1 if axis == axis_at else 1 for axis in range(len(dims))])
    return level


def routed_block(rng, own, number, rows, amount, top, reach, slope):
    ranking = jax.random.permutation(rng, amount)
    packed, ordinary = load_shares(amount, rows * top, reach, slope, True), load_shares(amount, rows * top, reach, slope, False)
    places = jnp.arange(amount)

    def named(tallies, rotation):
        used = int((tallies > 0).sum())
        fixed = max(1, used // 4)
        shifted = fixed + (places - fixed + rotation * (used - fixed)) % max(1, amount - fixed)
        return jnp.zeros((amount,), jnp.int32).at[ranking[jnp.where(places < fixed, places, shifted)]].set(jnp.asarray(tallies, jnp.int32))

    tallies = jnp.where(number % 4 == 0, named(packed, number // 4), named(ordinary, number - number // 4 - 1))
    mixed = jax.random.permutation(jax.random.fold_in(own, 3), amount)
    giver, taker = mixed[0:amount // 2 * 2:2], mixed[1:amount // 2 * 2:2]
    room = jnp.minimum(tallies[giver] - 1, reach - tallies[taker]) // 2
    room = jnp.where((giver == ranking[0]) | (taker == ranking[0]) | (tallies[taker] == 0), 0, jnp.maximum(room, 0))
    shifted = jax.random.randint(jax.random.fold_in(own, 4), (amount // 2,), 0, 1 << 20) % (room + 1)
    tallies = tallies.at[giver].add(-shifted).at[taker].add(shifted)
    members = jnp.searchsorted(jnp.cumsum(tallies), jnp.arange(rows * top), side="right").astype(jnp.int32)
    grid = members.reshape(top, rows).T
    grid = grid[jax.random.permutation(jax.random.fold_in(own, 1), rows)]
    rotation = jax.random.randint(jax.random.fold_in(own, 2), (rows, 1), 0, top)
    return jnp.take_along_axis(grid, (jnp.arange(top)[None, :] + rotation) % top, axis=1)


def load_shares(number_of, total, most, lean, full):
    weights = [(1 << 20) // math.isqrt(rank ** lean) + 1 for rank in range(1, number_of + 1)]
    largest = most if full else min(most, max(-(-total // number_of), total * weights[0] // sum(weights)))
    least = 1 if total - largest >= number_of - 1 else 0
    holding, spare = [largest] + [least] * (number_of - 1), total - largest - least * (number_of - 1)
    while spare > 0:
        free = [i for i in range(1, number_of) if holding[i] < largest] or [i for i in range(1, number_of) if holding[i] < most]
        mass, budget = sum([weights[i] for i in free]), spare
        for i in free:
            more = min(most - holding[i], max(1, budget * weights[i] // mass), spare)
            holding[i] = holding[i] + more
            spare = spare - more
    return np.array(holding)


def noise(stream_key, extent, width, reach, pieces=(), kind=jnp.bfloat16):
    array = width * jax.random.normal(stream_key, extent, jnp.float32)
    if pieces:
        array = array * steps_of(stream_key, extent, pieces, -0.22, 0.18)
    return jnp.clip(array, -reach, reach).astype(kind)


def setup_inputs(seed: int = 0) -> dict:
    streams_of = jax.random.split(jax.random.key(seed), 8)
    tokens = noise(streams_of[0], (TOKENS, D), 1.0, 6.0, ((0, 256),))
    expert_ids_keys = jax.random.split(jax.random.fold_in(streams_of[1], 1), TOKENS // TOK_DEV)
    expert_ids_turns = jax.random.permutation(jax.random.fold_in(streams_of[1], 3), TOKENS // TOK_DEV)
    expert_ids = jax.vmap(lambda own, number: routed_block(jax.random.fold_in(streams_of[1], 2), own, number, TOK_DEV, EXPERTS, TOPK, CAP, 2))(expert_ids_keys, expert_ids_turns).reshape((TOKENS, TOPK))
    gate_weights = jnp.clip(0.049804688 + 0.9501953 * jax.random.uniform(streams_of[2], (TOKENS, TOPK), jnp.float32) ** steps_of(streams_of[2], (TOKENS, TOPK), ((0, 256),), -0.2, 0.2), 0.049804688, 1.0).astype(jnp.bfloat16)
    w_gate = noise(streams_of[3], (EXPERTS, H, D), D ** -0.5, 0.09375, ((0, 64), (1, 4)))
    w_up = noise(streams_of[4], (EXPERTS, H, D), D ** -0.5, 0.09375, ((0, 64), (1, 4)))
    w_down = noise(streams_of[5], (EXPERTS, H, D), H ** -0.5, 0.21875, ((0, 64), (1, 4)))
    cotangent = noise(streams_of[6], (TOKENS, D), 0.25, 2.0, ((0, 256),))
    return dict(tokens=tokens, expert_ids=expert_ids, gate_weights=gate_weights, w_gate=w_gate, w_up=w_up, w_down=w_down, cotangent=cotangent)


block_rows = 128


def expert_terms(x_rows, dy_rows, gate_rows, gate_matrix, up_matrix, down_matrix):
    row_count = x_rows.shape[0]
    pre_gate = jnp.dot(x_rows, gate_matrix.T, preferred_element_type=jnp.float32)
    pre_up = jnp.dot(x_rows, up_matrix.T, preferred_element_type=jnp.float32)
    back = jnp.dot(dy_rows, down_matrix.T, preferred_element_type=jnp.float32)
    sigmoid_gate = jax.nn.sigmoid(pre_gate)
    silu_gate = pre_gate * sigmoid_gate
    activated = silu_gate * pre_up
    route_groups = jnp.sum((activated * back).reshape(row_count, N_SEQ, H_DEV), axis=2).astype(jnp.bfloat16)
    route_total = jnp.sum(route_groups.astype(jnp.float32), axis=1)
    gate_col = gate_rows.astype(jnp.float32)[:, None]
    scaled = (gate_col * activated).astype(jnp.bfloat16)
    gated_back = gate_col * back
    grad_pre_gate = (gated_back * pre_up * sigmoid_gate * (1.0 + pre_gate * (1.0 - sigmoid_gate))).astype(jnp.bfloat16)
    grad_pre_up = (gated_back * silu_gate).astype(jnp.bfloat16)
    grad_down = jnp.dot(scaled.T, dy_rows, preferred_element_type=jnp.float32)
    grad_gate = jnp.dot(grad_pre_gate.T, x_rows, preferred_element_type=jnp.float32)
    grad_up = jnp.dot(grad_pre_up.T, x_rows, preferred_element_type=jnp.float32)
    gate_groups = grad_pre_gate.astype(jnp.float32).reshape(row_count, N_SEQ, H_DEV)
    up_groups = grad_pre_up.astype(jnp.float32).reshape(row_count, N_SEQ, H_DEV)
    gate_parts = gate_matrix.astype(jnp.float32).reshape(N_SEQ, H_DEV, D)
    up_parts = up_matrix.astype(jnp.float32).reshape(N_SEQ, H_DEV, D)
    token_groups = (jnp.einsum("bsh,shd->bsd", gate_groups, gate_parts)
                    + jnp.einsum("bsh,shd->bsd", up_groups, up_parts)).astype(jnp.bfloat16)
    token_total = jnp.sum(token_groups.astype(jnp.float32), axis=1)
    return token_total, route_total, grad_gate, grad_up, grad_down


def reference(tokens, expert_ids, gate_weights, w_gate, w_up, w_down, cotangent):
    flat_ids = expert_ids.reshape(-1).astype(jnp.int32)
    flat_gates = gate_weights.reshape(-1)
    order = jnp.argsort(flat_ids, stable=True).astype(jnp.int32)
    counts = jnp.bincount(flat_ids, length=EXPERTS).astype(jnp.int32)
    starts = (jnp.cumsum(counts) - counts).astype(jnp.int32)
    order_padded = jnp.concatenate([order, jnp.zeros((block_rows,), jnp.int32)])

    def per_expert(carried, inputs):
        gate_matrix, up_matrix, down_matrix, first_pair, pair_count = inputs

        def one_block(block_index, state_now):
            dx_acc, route_acc, acc_gate, acc_up, acc_down = state_now
            offset = (block_index * block_rows).astype(jnp.int32)
            picked = lax.dynamic_slice_in_dim(order_padded, (first_pair + offset).astype(jnp.int32), block_rows)
            in_range = (offset + jnp.arange(block_rows, dtype=jnp.int32)) < pair_count
            token_rows = picked // TOPK
            gate_block = jnp.where(in_range, flat_gates[picked], jnp.zeros((), flat_gates.dtype))
            outcome = expert_terms(tokens[token_rows], cotangent[token_rows], gate_block,
                                   gate_matrix, up_matrix, down_matrix)
            dx_acc = dx_acc.at[token_rows].add(jnp.where(in_range[:, None], outcome[0], 0.0))
            route_acc = route_acc.at[picked].add(jnp.where(in_range, outcome[1], 0.0))
            return (dx_acc, route_acc, acc_gate + outcome[2], acc_up + outcome[3], acc_down + outcome[4])

        block_count = (pair_count + block_rows - 1) // block_rows
        empty = jnp.zeros((H, D), jnp.float32)
        finished = lax.fori_loop(0, block_count, one_block, (carried[0], carried[1], empty, empty, empty))
        grads_out = (finished[2].astype(jnp.bfloat16), finished[3].astype(jnp.bfloat16), finished[4].astype(jnp.bfloat16))
        return (finished[0], finished[1]), grads_out

    initial = (jnp.zeros((TOKENS, D), jnp.float32), jnp.zeros((TOKENS * TOPK,), jnp.float32))
    totals, grads_all = lax.scan(per_expert, initial, (w_gate, w_up, w_down, starts, counts))
    d_tokens = totals[0].astype(jnp.bfloat16)
    d_gates = totals[1].reshape(TOKENS, TOPK)
    return d_tokens, d_gates, grads_all[0], grads_all[1], grads_all[2]
```

```python
import jax
import jax.numpy as jnp
import numpy as np
from jax import lax
from jax.sharding import Mesh, PartitionSpec as P

CAP = 3
ZLO = 2
LANES = 128
COLUMN = ("seq", "zlo")
PLANE = ("y", "x", "core")
EXPERT = ("zlo", "y", "x", "core")
BF = jnp.bfloat16
F32 = jnp.float32


def dot(a, b, out=F32):
    return lax.dot_general(a, b, (((1,), (0,)), ((), ())), preferred_element_type=out)


def dot_t(a, b, out=F32):
    return lax.dot_general(a, b, (((1,), (1,)), ((), ())), preferred_element_type=out)


def tdot(a, b, out=F32):
    return lax.dot_general(a, b, (((0,), (0,)), ((), ())), preferred_element_type=out)


def column_gather(values, depth, me):
    got = [values]
    for far in range(1, depth):
        got.append(lax.ppermute(values, COLUMN, [(i, (i + far) % depth) for i in range(depth)]))
    picked = lax.rem(me - lax.iota(jnp.int32, depth) + depth, depth)
    return jnp.take(jnp.stack(got), picked, axis=0)


def per_device(tokens, expert_ids, gate_weights, w_gate, w_up, w_down, cotangent):
    groups = lax.axis_size("seq")
    plane = lax.axis_size(PLANE)
    depth = groups * ZLO
    experts = plane * ZLO
    rows, width = tokens.shape
    half = width // 2
    send = experts * CAP
    held = send * groups
    block = depth * CAP
    zlo = lax.axis_index("zlo")
    me = lax.axis_index("seq") * ZLO + zlo
    wg, wu, wd = w_gate[0], w_up[0], w_down[0]

    ids = expert_ids[:, 0]
    here = lax.iota(jnp.int32, rows)
    same = (ids[:, None] == ids[None, :]) & (here[None, :] < here[:, None])
    rank = jnp.sum(same.astype(jnp.int32), axis=1)
    slot = ids * CAP + rank
    to_slot = (slot[None, :] == lax.iota(jnp.int32, send)[:, None]).astype(BF)
    from_slot = (slot[:, None] == lax.iota(jnp.int32, send)[None, :]).astype(BF)

    x_column = lax.all_gather(tokens, COLUMN, axis=0, tiled=True)

    dy_send = dot(to_slot, cotangent, BF).reshape(experts, CAP, width)
    dy_mine = lax.all_to_all(dy_send, EXPERT, 0, 0, tiled=True).reshape(send, width)
    dy_held = lax.all_gather(dy_mine, "seq", axis=0, tiled=True)

    code = (ids % plane) * block + me * CAP + rank + held * (ids // plane)
    meta = jnp.stack([code.astype(F32), gate_weights[:, 0].astype(F32)])
    meta = column_gather(meta, depth, me)
    target = meta[:, 0, :].reshape(-1).astype(jnp.int32) - held * zlo
    gates_column = meta[:, 1, :].reshape(-1)
    in_column = depth * rows
    hit = target[None, :] == lax.iota(jnp.int32, held)[:, None]
    pick = hit.astype(BF)
    unpick = (target[:, None] == lax.iota(jnp.int32, held)[None, :]).astype(BF)
    gate_send = jnp.sum(jnp.where(hit, gates_column[None, :], 0.0), axis=1).reshape(plane, block)
    gate_x = lax.all_to_all(gate_send, PLANE, 0, 0, tiled=True).reshape(held)

    x_send = dot(pick, x_column, BF).reshape(plane, block, width)
    x_held = lax.all_to_all(x_send, PLANE, 0, 0, tiled=True).reshape(held, width)

    at = lax.iota(jnp.int32, held)
    as_x = (at % (plane * CAP)) // CAP * block + at // (plane * CAP) * CAP + at % CAP
    turn = as_x[:, None] == at[None, :]
    turn_bf = turn.astype(BF)
    turn_f32 = turn.astype(F32)
    pre_x = jnp.concatenate([dot_t(x_held, wg), dot_t(x_held, wu)], axis=1)
    pre = lax.dot_general(
        turn_f32, pre_x, (((1,), (0,)), ((), ())), precision=lax.Precision.HIGHEST,
        preferred_element_type=F32,
    )
    hidden = wg.shape[0]
    pre_gate, pre_up = pre[:, :hidden], pre[:, hidden:]
    gate_col = jnp.sum(jnp.where(turn, gate_x[None, :], 0.0), axis=1)[:, None]

    back = dot_t(dy_held, wd)
    sigmoid_gate = jax.nn.sigmoid(pre_gate)
    silu_gate = pre_gate * sigmoid_gate
    activated = silu_gate * pre_up
    route = jnp.sum(activated * back, axis=1, keepdims=True).astype(BF)
    scaled = (gate_col * activated).astype(BF)
    gated_back = gate_col * back
    g_gate = (gated_back * pre_up * sigmoid_gate * (1.0 + pre_gate * (1.0 - sigmoid_gate))).astype(BF)
    g_up = (gated_back * silu_gate).astype(BF)

    part_a = (dot(g_gate, wg[:, :half]) + dot(g_up, wu[:, :half])).astype(BF)
    sum_a = lax.psum_scatter(part_a, "seq", scatter_dimension=0, tiled=True)

    g_gate_x = tdot(turn_bf, g_gate, BF)
    g_up_x = tdot(turn_bf, g_up, BF)
    route_x = tdot(turn_bf, jnp.broadcast_to(route, (held, LANES)), BF)
    part_b = (dot(g_gate_x, wg[:, half:]) + dot(g_up_x, wu[:, half:])).astype(BF)
    part_b = jnp.concatenate([part_b, route_x], axis=1)
    back_b = lax.all_to_all(part_b.reshape(plane, block, half + LANES), PLANE, 0, 0, tiled=True)
    column_b = dot(unpick, back_b.reshape(held, half + LANES), BF)
    sum_b = lax.psum_scatter(column_b, COLUMN, scatter_dimension=0, tiled=True)

    back_a = lax.all_to_all(sum_a.reshape(experts, CAP, half), EXPERT, 0, 0, tiled=True)
    rows_a = dot(from_slot, back_a.reshape(send, half), BF)

    grad_gate = tdot(g_gate_x, x_held, BF)
    grad_up = tdot(g_up_x, x_held, BF)
    grad_down = tdot(scaled, dy_held, BF)

    d_tokens = jnp.concatenate([rows_a, sum_b[:, :half]], axis=1)
    d_gates = sum_b[:, half:half + 1].astype(F32)
    return (d_tokens, d_gates, grad_gate[None], grad_up[None], grad_down[None])


def solution(mesh):
    groups, experts = mesh.shape["seq"], mesh.shape["expert"]
    side = int(np.sqrt(experts // (2 * ZLO)))
    fine = Mesh(
        np.asarray(mesh.devices).reshape(groups, ZLO, experts // (2 * ZLO * side), side, 2),
        ("seq", "zlo", "y", "x", "core"),
    )
    by_row = P(("seq",) + EXPERT, None)
    by_expert = P(EXPERT, "seq", None)
    return jax.shard_map(
        per_device,
        mesh=fine,
        in_specs=(by_row, by_row, by_row, by_expert, by_expert, by_expert, by_row),
        out_specs=(by_row, by_row, by_expert, by_expert, by_expert),
        check_vma=False,
    )
```

```python
import jax
import jax.numpy as jnp
import numpy as np
from jax import lax
from jax.sharding import Mesh, PartitionSpec as P

CAP = 3
ZLO = 2
LANES = 128
COLUMN = ("seq", "zlo")
PLANE = ("y", "x", "core")
EXPERT = ("zlo", "y", "x", "core")
BF = jnp.bfloat16
F32 = jnp.float32


def dot(a, b, out=F32):
    return lax.dot_general(a, b, (((1,), (0,)), ((), ())), preferred_element_type=out)


def dot_t(a, b, out=F32):
    return lax.dot_general(a, b, (((1,), (1,)), ((), ())), preferred_element_type=out)


def tdot(a, b, out=F32):
    return lax.dot_general(a, b, (((0,), (0,)), ((), ())), preferred_element_type=out)


def shift(value, axis, count, by):
    return lax.ppermute(value, axis, [(i, (i + by) % count) for i in range(count)])


def ring_gather(parts, axis, count):
    got = [{0: parts[0]}, {0: parts[1]}]
    ahead, behind = list(parts), list(parts)
    for step in range(1, count // 2):
        for part in range(2):
            ahead[part] = shift(ahead[part], axis, count, 1)
            behind[part] = shift(behind[part], axis, count, -1)
            got[part][step] = ahead[part]
            got[part][count - step] = behind[part]
    got[0][count // 2] = shift(ahead[0], axis, count, 1)
    got[1][count // 2] = shift(behind[1], axis, count, -1)
    return got


def ring_scatter(block, axis, count):
    def total(value, carried):
        return value if carried is None else value + carried.astype(F32)

    far = count // 2
    ahead = [shift(block(far, 0).astype(BF), axis, count, 1), None]
    behind = [None, shift(block(far, 1).astype(BF), axis, count, -1)]
    for step in range(far - 1, 0, -1):
        for part in range(2):
            other = 1 - part
            ahead[other] = shift(total(block(count - step, other), ahead[other]).astype(BF), axis, count, 1)
            behind[part] = shift(total(block(step, part), behind[part]).astype(BF), axis, count, -1)
    return [total(total(block(0, part), ahead[part]), behind[part]) for part in range(2)]


def per_device(tokens, expert_ids, gate_weights, w_gate, w_up, w_down, cotangent):
    groups = lax.axis_size("seq")
    plane = lax.axis_size(PLANE)
    depth = groups * ZLO
    experts = plane * ZLO
    rows, width = tokens.shape
    half = width // 2
    send = experts * CAP
    held = send * groups
    block = depth * CAP
    zlo = lax.axis_index("zlo")
    group = lax.axis_index("seq")
    me = group * ZLO + zlo
    wg, wu, wd = w_gate[0], w_up[0], w_down[0]
    hidden = wg.shape[0]

    ids = expert_ids[:, 0]
    here = lax.iota(jnp.int32, rows)
    same = (ids[:, None] == ids[None, :]) & (here[None, :] < here[:, None])
    rank = jnp.sum(same.astype(jnp.int32), axis=1)
    slot = ids * CAP + rank
    from_slot = (slot[:, None] == lax.iota(jnp.int32, send)[None, :]).astype(BF)

    part_rows = rows // 2
    notes = jnp.stack(
        [slot[:part_rows].astype(BF), slot[part_rows:].astype(BF),
         gate_weights[:part_rows, 0], gate_weights[part_rows:, 0]], axis=1)
    notes = jnp.pad(notes, ((0, 0), (0, LANES - 4)))
    second = jnp.concatenate([tokens[part_rows:], notes], axis=1)
    x_got = ring_gather([tokens[:part_rows], second], COLUMN, depth)

    dy_send = tdot(from_slot, cotangent, BF).reshape(experts, CAP, width)
    dy_mine = lax.all_to_all(dy_send, EXPERT, 0, 0, tiled=True).reshape(send, width)
    dy_got = ring_gather([dy_mine[:send // 2], dy_mine[send // 2:]], "seq", groups)
    dy_held = jnp.concatenate([dy_got[part][d] for d in range(groups) for part in range(2)], axis=0)

    def places(d, part):
        noted = x_got[1][d][:, width:width + 4].astype(F32)
        slots = noted[:, part].astype(jnp.int32)
        of = slots // CAP
        row = (of % plane) * block + lax.rem(me - d + depth, depth) * CAP + slots % CAP
        return jnp.where(of // plane == zlo, row, -1), noted[:, 2 + part]

    order = [(d, part) for d in (*range(0, depth // 2 - 1), *range(depth // 2 + 2, depth)) for part in range(2)]
    late = [(d, part) for d in (depth // 2 - 1, depth // 2 + 1, depth // 2) for part in range(2)]
    at = lax.iota(jnp.int32, held)
    unpick, gate_send, x_send = {}, 0.0, []
    for keys in (order, late):
        noted = [places(*key) for key in keys]
        hits = jnp.concatenate([n[0] for n in noted])[:, None] == at[None, :]
        gates = jnp.concatenate([n[1] for n in noted])[:, None]
        gate_send = gate_send + jnp.sum(jnp.where(hits, gates, 0.0), axis=0)
        rows_in = jnp.concatenate([x_got[part][d][:, :width] for d, part in keys], axis=0)
        x_send.append(tdot(hits.astype(BF), rows_in))
        for key, n in zip(keys, noted):
            unpick[key] = n[0]
    x_send = (x_send[0].astype(BF).astype(F32) + x_send[1]).astype(BF)
    x_held = lax.all_to_all(x_send.reshape(plane, block, width), PLANE, 0, 0, tiled=True).reshape(held, width)
    gate_x = lax.all_to_all(gate_send.reshape(plane, block), PLANE, 0, 0, tiled=True).reshape(held)

    of_group = lax.rem(group - at // send + groups, groups)
    of_zlo = at % send // (plane * CAP)
    as_x = at % (plane * CAP) // CAP * block + (of_group * ZLO + of_zlo) * CAP + at % CAP
    turn = as_x[:, None] == at[None, :]
    turn_bf = turn.astype(BF)
    w_both = jnp.concatenate([wg, wu], axis=0)
    pre = lax.dot_general(
        turn.astype(F32), dot_t(x_held, w_both), (((1,), (0,)), ((), ())), precision=lax.Precision.HIGHEST,
        preferred_element_type=F32,
    )
    pre_gate, pre_up = pre[:, :hidden], pre[:, hidden:]
    gate_col = jnp.sum(jnp.where(turn, gate_x[None, :], 0.0), axis=1)[:, None]

    back = dot_t(dy_held, wd)
    sigmoid_gate = jax.nn.sigmoid(pre_gate)
    silu_gate = pre_gate * sigmoid_gate
    activated = silu_gate * pre_up
    route = jnp.sum(activated * back, axis=1, keepdims=True).astype(BF)
    scaled = (gate_col * activated).astype(BF)
    gated_back = gate_col * back
    g_gate = (gated_back * pre_up * sigmoid_gate * (1.0 + pre_gate * (1.0 - sigmoid_gate))).astype(BF)
    g_up = (gated_back * silu_gate).astype(BF)
    g_both = jnp.concatenate([g_gate, g_up], axis=1)

    w_a = w_both[:, :half]
    part_send = send // 2

    def block_a(d, part):
        first = d * send + part * part_send
        return dot(g_both[first:first + part_send], w_a)

    sum_a = jnp.concatenate([s.astype(BF) for s in ring_scatter(block_a, "seq", groups)], axis=0)

    g_x = tdot(turn_bf, jnp.concatenate([g_both, jnp.pad(route, ((0, 0), (0, LANES - 1)))], axis=1), BF)
    w_b = jnp.pad(w_both[:, half:], ((0, LANES), (0, LANES)))
    route_at = (lax.broadcasted_iota(jnp.int32, w_b.shape, 0) == 2 * hidden) & (
        lax.broadcasted_iota(jnp.int32, w_b.shape, 1) == half)
    w_b = jnp.where(route_at, jnp.ones((), BF), w_b)
    part_b = dot(g_x, w_b, BF)
    back_b = lax.all_to_all(part_b.reshape(plane, block, half + LANES), PLANE, 0, 0, tiled=True)
    back_b = back_b.reshape(held, half + LANES)

    def block_b(d, part):
        return dot((unpick[d, part][:, None] == at[None, :]).astype(BF), back_b)

    sum_b = jnp.concatenate(ring_scatter(block_b, COLUMN, depth), axis=0)

    back_a = lax.all_to_all(sum_a.reshape(experts, CAP, half), EXPERT, 0, 0, tiled=True)
    rows_a = dot(from_slot, back_a.reshape(send, half), BF)

    grad_gate = tdot(g_x[:, :hidden], x_held, BF)
    grad_up = tdot(g_x[:, hidden:2 * hidden], x_held, BF)
    grad_down = tdot(scaled, dy_held, BF)

    d_tokens = jnp.concatenate([rows_a, sum_b[:, :half].astype(BF)], axis=1)
    d_gates = sum_b[:, half:half + 1]
    return (d_tokens, d_gates, grad_gate[None], grad_up[None], grad_down[None])


def solution(mesh):
    groups, experts = mesh.shape["seq"], mesh.shape["expert"]
    side = int(np.sqrt(experts // (2 * ZLO)))
    fine = Mesh(
        np.asarray(mesh.devices).reshape(groups, ZLO, experts // (2 * ZLO * side), side, 2),
        ("seq", "zlo", "y", "x", "core"),
    )
    by_row = P(("seq",) + EXPERT, None)
    by_expert = P(EXPERT, "seq", None)
    return jax.shard_map(
        per_device,
        mesh=fine,
        in_specs=(by_row, by_row, by_row, by_expert, by_expert, by_expert, by_row),
        out_specs=(by_row, by_row, by_expert, by_expert, by_expert),
        check_vma=False,
    )
```

```python
import jax
import jax.numpy as jnp
import numpy as np
from jax import lax
from jax.sharding import Mesh, PartitionSpec as P

CAP = 3
ZLO = 2
LANES = 128
COLUMN = ("seq", "zlo")
PLANE = ("y", "x", "core")
EXPERT = ("zlo", "y", "x", "core")
BF = jnp.bfloat16
F32 = jnp.float32


def dot(a, b, out=F32):
    return lax.dot_general(a, b, (((1,), (0,)), ((), ())), preferred_element_type=out)


def dot_t(a, b, out=F32):
    return lax.dot_general(a, b, (((1,), (1,)), ((), ())), preferred_element_type=out)


def tdot(a, b, out=F32):
    return lax.dot_general(a, b, (((0,), (0,)), ((), ())), preferred_element_type=out)


def per_device(tokens, expert_ids, gate_weights, w_gate, w_up, w_down, cotangent):
    groups = lax.axis_size("seq")
    plane = lax.axis_size(PLANE)
    depth = groups * ZLO
    experts = plane * ZLO
    rows, width = tokens.shape
    half = width // 2
    send = experts * CAP
    held = send * groups
    block = depth * CAP
    zlo = lax.axis_index("zlo")
    wg, wu, wd = w_gate[0], w_up[0], w_down[0]

    ids = expert_ids[:, 0]
    here = lax.iota(jnp.int32, rows)
    same = (ids[:, None] == ids[None, :]) & (here[None, :] < here[:, None])
    rank = jnp.sum(same.astype(jnp.int32), axis=1)
    slot = ids * CAP + rank
    to_slot = (slot[None, :] == lax.iota(jnp.int32, send)[:, None]).astype(BF)
    from_slot = (slot[:, None] == lax.iota(jnp.int32, send)[None, :]).astype(BF)

    notes = jnp.pad(jnp.stack([slot.astype(BF), gate_weights[:, 0]], axis=1), ((0, 0), (0, LANES - 2)))
    x_column = lax.all_gather(jnp.concatenate([tokens, notes], axis=1), COLUMN, axis=0, tiled=True)
    dy_send = dot(to_slot, cotangent, BF).reshape(experts, CAP, width)
    dy_mine = lax.all_to_all(dy_send, EXPERT, 0, 0, tiled=True).reshape(send, width)

    slots = x_column[:, width].astype(jnp.int32)
    to = slots // CAP
    source = lax.iota(jnp.int32, depth * rows) // rows
    target = jnp.where(to // plane == zlo, to % plane * block + source * CAP + slots % CAP, -1)
    pick = (target[None, :] == lax.iota(jnp.int32, held)[:, None]).astype(BF)
    unpick = (target[:, None] == lax.iota(jnp.int32, held)[None, :]).astype(BF)

    def choose(column):
        return dot(pick, column, BF).reshape(plane, block, column.shape[1])

    def to_expert(chosen):
        return lax.all_to_all(chosen, PLANE, 0, 0, tiled=True).reshape(held, chosen.shape[2])

    dy_held = lax.all_gather(dy_mine, "seq", axis=0, tiled=True)
    x_held = to_expert(choose(x_column))
    gate_x = x_held[:, width + 1].astype(F32)
    x_held = x_held[:, :width]

    at = lax.iota(jnp.int32, held)
    as_x = (at % (plane * CAP)) // CAP * block + at // (plane * CAP) * CAP + at % CAP
    turn = as_x[:, None] == at[None, :]
    turn_bf = turn.astype(BF)
    turn_f32 = turn.astype(F32)

    def turned(value):
        return lax.dot_general(
            turn_f32, value, (((1,), (0,)), ((), ())), precision=lax.Precision.HIGHEST, preferred_element_type=F32,
        )

    w_both = jnp.concatenate([wg, wu], axis=0)
    pre = turned(dot_t(x_held, w_both))
    hidden = wg.shape[0]
    pre_gate, pre_up = pre[:, :hidden], pre[:, hidden:]
    gate_col = jnp.sum(jnp.where(turn, gate_x[None, :], 0.0), axis=1)[:, None]

    back = dot_t(dy_held, wd)
    sigmoid_gate = jax.nn.sigmoid(pre_gate)
    silu_gate = pre_gate * sigmoid_gate
    activated = silu_gate * pre_up
    route = jnp.sum(activated * back, axis=1, keepdims=True).astype(BF)
    scaled = (gate_col * activated).astype(BF)
    gated_back = gate_col * back
    g_gate = (gated_back * pre_up * sigmoid_gate * (1.0 + pre_gate * (1.0 - sigmoid_gate))).astype(BF)
    g_up = (gated_back * silu_gate).astype(BF)

    part_a = (dot(g_gate, wg[:, :half]) + dot(g_up, wu[:, :half])).astype(BF)
    sum_a = lax.psum_scatter(part_a, "seq", scatter_dimension=0, tiled=True)

    g_gate_x = tdot(turn_bf, g_gate, BF)
    g_up_x = tdot(turn_bf, g_up, BF)
    route_x = tdot(turn_bf, jnp.broadcast_to(route, (held, LANES)), BF)
    part_b = (dot(g_gate_x, wg[:, half:]) + dot(g_up_x, wu[:, half:])).astype(BF)
    part_b = jnp.concatenate([part_b, route_x], axis=1)
    back_b = lax.all_to_all(part_b.reshape(plane, block, half + LANES), PLANE, 0, 0, tiled=True)
    column_b = dot(unpick, back_b.reshape(held, half + LANES), BF)
    sum_b = lax.psum_scatter(column_b, COLUMN, scatter_dimension=0, tiled=True)

    back_a = lax.all_to_all(sum_a.reshape(experts, CAP, half), EXPERT, 0, 0, tiled=True)
    rows_a = dot(from_slot, back_a.reshape(send, half), BF)

    grad_gate = tdot(g_gate_x, x_held, BF)
    grad_up = tdot(g_up_x, x_held, BF)
    grad_down = tdot(scaled, dy_held, BF)

    d_tokens = jnp.concatenate([rows_a, sum_b[:, :half]], axis=1)
    d_gates = sum_b[:, half:half + 1].astype(F32)
    return (d_tokens, d_gates, grad_gate[None], grad_up[None], grad_down[None])


def solution(mesh):
    groups, experts = mesh.shape["seq"], mesh.shape["expert"]
    side = int(np.sqrt(experts // (2 * ZLO)))
    fine = Mesh(
        np.asarray(mesh.devices).reshape(groups, ZLO, experts // (2 * ZLO * side), side, 2),
        ("seq", "zlo", "y", "x", "core"),
    )
    by_row = P(("seq",) + EXPERT, None)
    by_expert = P(EXPERT, "seq", None)
    return jax.shard_map(
        per_device,
        mesh=fine,
        in_specs=(by_row, by_row, by_row, by_expert, by_expert, by_expert, by_row),
        out_specs=(by_row, by_row, by_expert, by_expert, by_expert),
        check_vma=False,
    )
```
